128 devices in a mesh: gz: 8 (over z_lo, x), gx: 16 (over y, z_hi, core).
Axes of the slice: x: 4, y: 4, z: 4 (z_hi: 2, z_lo: 2; z = z_hi * 2 + z_lo), core: 2. Of those that a mesh axis runs over, the one named last changes fastest.
Arguments:
- adj_fields: float32 [6, 256, 256, 8, 128], P(None, 'gx', 'gz'), may hold values from -6 to 6
- coef_e: float32 [256, 256, 8, 128], P('gx', 'gz'), may hold values from 0.1 to 0.6
- plane_z: int32 [2], replicated, may hold values from 0 to 255
- snap_index: int32 [1], replicated, may hold values from 0 to 2
- fwd_snaps: float32 [4, 2, 3, 256, 1024], P(None, None, None, 'gx', 'gz'), may hold values from -6 to 6
- design: float32 [2, 256, 1024], P(None, 'gx', 'gz'), may hold values from 0 to 1
- sens_in: float32 [2, 256, 1024], P(None, 'gx', 'gz'), may hold values from -6 to 6
Outputs:
- new_fields: float32 [6, 256, 256, 8, 128], P(None, 'gx', 'gz')
- gradient: float32 [2, 256, 1024], P(None, 'gx', 'gz')
The draws below stay inside these ranges and needn't reach their ends.
Inputs may be any that keep to these rules, and one draw needn't show every extreme that they name: `plane_z`: the two design planes may lie in the same or in different z slabs.
All inputs are finite; a program needn't handle non-finite values.
Results may differ from the reference program's by a relative error of at most 0.00016.
Values sent between devices are 32-bit elements; how exact they have to be, the bound alone decides.
No kernel may reach another device: no remote copies, remote signals or barrier semaphores. Data moves between devices by JAX's collectives and lax.ppermute only.
A program may use at most 128 MiB of HBM per device.

```python
import math
import jax
import jax.numpy as jnp
from jax import lax

NY = 1024
R = 8
STEPS = 2
SNAP = 4
NX = 256
NZ = 256


def shard_levels(stream_key, extent, cuts, least, top_value):
    level = 1.0
    for dim, shards_of in cuts:
        draws = jax.random.uniform(jax.random.fold_in(jax.random.fold_in(stream_key, 6), dim), (shards_of,), jnp.float32, least / len(cuts), top_value / len(cuts))
        level = level * jnp.repeat(jnp.exp(draws), extent[dim] // shards_of).reshape((-1,) + (1,) * (len(extent) - 1 - dim))
    return level


def gaussian(stream_key, dims, scale, limit, split=(), kind=jnp.bfloat16):
    drawn = scale * jax.random.normal(stream_key, dims, jnp.float32)
    if split:
        drawn = drawn * shard_levels(stream_key, dims, split, -0.22, 0.18)
    return jnp.clip(drawn, -limit, limit).astype(kind)


def setup_inputs(seed: int = 0) -> dict:
    streams_of = jax.random.split(jax.random.key(seed), 8)
    adj_fields = gaussian(streams_of[0], (6, NX, NZ, NY // 128, 128), 1.0, 6.0, ((1, 16), (2, 8)), jnp.float32)
    coef_e = jnp.clip(jnp.exp(math.log(0.6) - 1.7917595 * jax.random.uniform(streams_of[1], (NX, NZ, NY // 128, 128), jnp.float32) ** shard_levels(streams_of[1], (NX, NZ, NY // 128, 128), ((0, 16), (1, 8)), -0.2, 0.2)), 0.1, 0.6)
    plane_z = jax.random.randint(streams_of[2], (2,), 0, NZ).astype(jnp.int32)
    snap_index = jax.random.randint(streams_of[3], (1,), 0, SNAP - STEPS + 1).astype(jnp.int32)
    fwd_snaps = gaussian(streams_of[4], (SNAP, 2, 3, NX, NY), 1.0, 6.0, ((3, 16), (4, 8)), jnp.float32)
    design = jnp.clip(1.0 * jax.random.uniform(streams_of[5], (2, NX, NY), jnp.float32) ** shard_levels(streams_of[5], (2, NX, NY), ((1, 16), (2, 8)), -0.2, 0.2), 0.0, 1.0)
    sens_in = gaussian(streams_of[6], (2, NX, NY), 1.0, 6.0, ((1, 16), (2, 8)), jnp.float32)
    return dict(adj_fields=adj_fields, coef_e=coef_e, plane_z=plane_z, snap_index=snap_index, fwd_snaps=fwd_snaps, design=design, sens_in=sens_in)


magnetic_step = 0.5
sharpness = 8.0
threshold = 0.5

def cone_table(radius):
    raw = [[max(0.0, radius - math.sqrt((first - radius) ** 2 + (second - radius) ** 2)) for second in range(2 * radius + 1)] for first in range(2 * radius + 1)]
    total = sum((sum(line) for line in raw))
    return [[entry / total for entry in line] for line in raw]

def forward(component, direction):
    widths = [(0, 1) if number == direction else (0, 0) for number in range(3)]
    padded = jnp.pad(component, widths)
    return lax.slice_in_dim(padded, 1, None, axis=direction) - component

def backward(component, direction):
    widths = [(1, 0) if number == direction else (0, 0) for number in range(3)]
    padded = jnp.pad(component, widths)
    return component - lax.slice_in_dim(padded, 0, component.shape[direction], axis=direction)

def cone_filter(values):
    weights_table = cone_table(R)
    padded = jnp.pad(values, ((0, 0), (R, R), (R, R)))
    row_count, col_count = (values.shape[1], values.shape[2])
    filtered_sum = jnp.zeros(values.shape, jnp.float32)
    for offset_x in range(2 * R + 1):
        for offset_y in range(2 * R + 1):
            weight = weights_table[offset_x][offset_y]
            filtered_sum = filtered_sum + weight * padded[:, offset_x:offset_x + row_count, offset_y:offset_y + col_count]
    return filtered_sum

def projection_slope(filtered):
    scale_down = math.tanh(sharpness * threshold) + math.tanh(sharpness * (1.0 - threshold))
    return sharpness * (1.0 - jnp.tanh(sharpness * (filtered - threshold)) ** 2) / scale_down

def reference(adj_fields, coef_e, plane_z, snap_index, fwd_snaps, design, sens_in):
    flat_fields = adj_fields.reshape(6, NX, NZ, NY)
    flat_coef = coef_e.reshape(NX, NZ, NY)
    electric = flat_fields[0:3]
    magnetic = flat_fields[3:6]
    sensitivity = sens_in
    for step in range(STEPS):
        electric_x, electric_y, electric_z = (electric[0], electric[1], electric[2])
        rotation = jnp.stack([forward(electric_z, 2) - forward(electric_y, 1), forward(electric_x, 1) - forward(electric_z, 0), forward(electric_y, 0) - forward(electric_x, 2)])
        magnetic = magnetic + magnetic_step * rotation
        magnetic_x, magnetic_y, magnetic_z = (magnetic[0], magnetic[1], magnetic[2])
        rotation_back = jnp.stack([backward(magnetic_z, 2) - backward(magnetic_y, 1), backward(magnetic_x, 1) - backward(magnetic_z, 0), backward(magnetic_y, 0) - backward(magnetic_x, 2)])
        electric = electric - flat_coef[None] * rotation_back
        snapshot = lax.dynamic_index_in_dim(fwd_snaps, (snap_index[0] + step).astype(jnp.int32), 0, keepdims=False)
        layers = jnp.stack([lax.dynamic_index_in_dim(electric, plane_z[plane_index].astype(jnp.int32), 2, keepdims=False) for plane_index in range(2)])
        sensitivity = sensitivity + lax.optimization_barrier(jnp.sum(snapshot * layers, axis=1))
    filtered = cone_filter(design)
    gradient = cone_filter(sensitivity * projection_slope(filtered))
    new_fields = jnp.concatenate([electric, magnetic], axis=0).reshape(6, NX, NZ, NY // 128, 128)
    return (new_fields, gradient)
```

```python
import functools
import math

import jax
import jax.numpy as jnp
from jax import lax
from jax.experimental import pallas as pl
from jax.experimental.pallas import tpu as pltpu
from jax.sharding import PartitionSpec as P

R = 8
STEPS = 2
SHARPNESS = 8.0
THRESHOLD = 0.5
HALF = 0.5
F32 = jnp.float32
SUB, LANE = 8, 128
CHUNK = 32
SLOT = 16

VMEM = pl.BlockSpec(memory_space=pltpu.VMEM)
HBM = pl.BlockSpec(memory_space=pltpu.HBM)
SMEM = pl.BlockSpec(memory_space=pltpu.SMEM)


def weight(a, b):
    total = sum(
        max(0.0, R - math.sqrt(i * i + j * j)) for i in range(-R, R + 1) for j in range(-R, R + 1)
    )
    return max(0.0, R - math.sqrt(a * a + b * b)) / total


def call(kernel, outs, ins, out_specs=None, in_specs=None, scratch=(), alias=None, cost=None, limit=8):
    out_specs = out_specs or [VMEM] * len(outs)
    in_specs = in_specs or [VMEM] * len(ins)
    return pl.pallas_call(
        kernel,
        out_shape=outs,
        in_specs=in_specs,
        out_specs=out_specs,
        scratch_shapes=list(scratch),
        input_output_aliases=alias or {},
        cost_estimate=cost,
        compiler_params=pltpu.CompilerParams(vmem_limit_bytes=limit << 20),
    )(*ins)


def vmem(*shape):
    return pltpu.VMEM(shape, F32)


def is_even(axis):
    return lax.rem(lax.axis_index(axis), 2) == 0


def iota(v, dim):
    return lax.broadcasted_iota(jnp.int32, v.shape, dim)


def ahead(v):
    n = v.ndim
    r = pltpu.roll(v, LANE - 1, n - 1)
    s = jnp.where(iota(v, n - 2) == SUB - 1, 0.0, pltpu.roll(r, SUB - 1, n - 2))
    return jnp.where(iota(v, n - 1) == LANE - 1, s, r)


def behind(v):
    n = v.ndim
    r = pltpu.roll(v, 1, n - 1)
    s = jnp.where(iota(v, n - 2) == 0, 0.0, pltpu.roll(r, 1, n - 2))
    return jnp.where(iota(v, n - 1) == 0, s, r)


def part_z(ex, ey, ez, hx, hy, ez_next, out, x_cells):
    out[0:x_cells] = hx + HALF * ((ahead(ez) - ez) + ey)
    out[x_cells : 2 * x_cells] = hy + HALF * (-ex - (ez_next - ez))


def part_x(ex, exz, ey, ez, hy, hz):
    return hy + HALF * ((exz - ex) + ez), hz + HALF * (-ey - (ahead(ex) - ex))


def post(first, second, even, rows, forward, backward):
    first[rows] = jnp.where(even, forward, backward)
    second[rows] = jnp.where(even, backward, forward)


def pack_slots(arrays, trailing):
    per = LANE // SLOT
    tiles = []
    for t in range(-(-len(arrays) // per)):
        group = arrays[t * per : (t + 1) * per]
        lane = iota(group[0], 1)
        tile = jnp.zeros_like(group[0])
        for k, v in enumerate(group):
            shift = (SLOT * k + (SLOT if trailing else 0)) % LANE
            moved = pltpu.roll(v, shift, 1) if shift else v
            tile = jnp.where((lane >= SLOT * k) & (lane < SLOT * (k + 1)), moved, tile)
        tiles.append(tile)
    return tiles


def unpack_slot(left_tile, right_tile, k):
    lane = iota(left_tile, 1)
    right = pltpu.roll(right_tile, (LANE - SLOT * k) % LANE, 1) if k else right_tile
    shift = (LANE - SLOT - SLOT * k) % LANE
    left = pltpu.roll(left_tile, shift, 1) if shift else left_tile
    return jnp.where(lane < SLOT, right, jnp.where(lane >= LANE - SLOT, left, 0.0))


def rows_of(v):
    return v.reshape(v.shape[0] // SUB, SUB, LANE)


def flat(v):
    return v.reshape(v.shape[0] * SUB, LANE)


def open_kernel(f, design, sens, snaps, snap_index, za, zb, xa, xb, lo, hi, first, last, sem):
    cells_x, cells_z = f.shape[1], f.shape[2]
    copies = [
        pltpu.make_async_copy(f.at[0:2, :, 0], lo, sem.at[0]),
        pltpu.make_async_copy(f.at[0:5, :, cells_z - 1], hi, sem.at[1]),
        pltpu.make_async_copy(f.at[1:3, 0], first, sem.at[2]),
        pltpu.make_async_copy(f.at[:, cells_x - 1], last, sem.at[3]),
    ]
    for c in copies:
        c.start()
    even_z, even_x = is_even("gz"), is_even("gx")
    s0 = snap_index[0]
    arrays = [design[0], design[1], sens[0], sens[1]]
    arrays += [snaps[s0 + s, p, c] for s in range(STEPS) for p in range(2) for c in range(3)]
    base = 2 * cells_x + 1
    tiles = zip(pack_slots(arrays, True), pack_slots(arrays, False))
    for t, (forward, backward) in enumerate(tiles):
        n = forward.shape[0] // SUB
        post(za, zb, even_z, pl.ds(base + n * t, n), rows_of(forward), rows_of(backward))
    copies[0].wait()
    copies[1].wait()
    z_rows(lo[0], lo[1], hi, za, zb, even_z, cells_x)
    copies[2].wait()
    copies[3].wait()
    x_rows(first, 0, last, xa, xb, even_x, cells_z)


def z_rows(ex0, ey0, hi, za, zb, even, cells_x):
    ex, ey, ez, hx, hy = (hi[c] for c in range(5))
    ez_next = jnp.concatenate([ez[1:], jnp.zeros_like(ez[:1])], axis=0)
    bx = hx + HALF * ((ahead(ez) - ez) + ey)
    by = hy + HALF * (-ex - (ez_next - ez))
    post(za, zb, even, pl.ds(0, cells_x), bx, ex0)
    post(za, zb, even, pl.ds(cells_x, cells_x), by, ey0)
    za[2 * cells_x] = ez[0]
    zb[2 * cells_x] = ez[0]


def x_rows(first, offset, last, xa, xb, even, cells_z):
    for z in range(0, cells_z, 8):
        n = pl.ds(z, 8)
        ex, ey, ez, hy, hz = (last[c, pl.ds(z + offset, 8)] for c in (0, 1, 2, 4, 5))
        if z + 8 < cells_z:
            exz = last[0, pl.ds(z + offset + 1, 8)]
        else:
            exz = jnp.concatenate([ex[1:], jnp.zeros_like(ex[:1])], axis=0)
        ay, az = part_x(ex, exz, ey, ez, hy, hz)
        post(xa, xb, even, n, ay, first[0, pl.ds(z + offset, 8)])
        post(xa, xb, even, pl.ds(cells_z + z, 8), az, first[1, pl.ds(z + offset, 8)])
    line = pl.ds(2 * cells_z, 1)
    xa[line] = jnp.zeros_like(xa[line])
    xb[line] = jnp.zeros_like(xb[line])


def patch_kernel(cells_x, cells_z, with_design, *refs):
    if with_design:
        za, zb, design, xa, xb, xao, xbo = refs
    else:
        za, zb, xa, xb, xao, xbo = refs
    even_z, even_x = is_even("gz"), is_even("gx")
    rows = 2 * cells_z + 1
    for r in range(0, 2 * cells_z, 8):
        xao[pl.ds(r, 8)] = xa[pl.ds(r, 8)]
        xbo[pl.ds(r, 8)] = xb[pl.ds(r, 8)]
    corner = HALF * jnp.where(even_z, za[cells_x - 1], zb[cells_x - 1])
    last = cells_z - 1
    xao[last] = xa[last] + jnp.where(even_x, corner, 0.0)
    xbo[last] = xb[last] + jnp.where(even_x, 0.0, corner)
    line = jnp.where(even_z, zb[2 * cells_x], za[2 * cells_x])
    xao[2 * cells_z] = line
    xbo[2 * cells_z] = line
    if with_design:
        base = 2 * cells_x + 1
        n = cells_x // SUB
        tile_a, tile_b = flat(za[pl.ds(base, n)]), flat(zb[pl.ds(base, n)])
        right = jnp.where(even_z, tile_a, tile_b)
        left = jnp.where(even_z, tile_b, tile_a)
        for p in range(2):
            own = rows_of(design[p])
            halo = rows_of(unpack_slot(left, right, p))
            for o, v in ((0, own), (n, halo)):
                xao[pl.ds(rows + 2 * n * p + o, n)] = v
                xbo[pl.ds(rows + 2 * n * p + o, n)] = v


def update_plane(s, coef, i, electric, cells_z):
    def chunk(k, carry):
        hx_prev, hy_prev = carry
        z = 1 + CHUNK * k
        zs = pl.ds(z, CHUNK)
        ex, ey, ez = s[0, i, zs], s[1, i, zs], s[2, i, zs]
        exz = jnp.concatenate([ex[1:], s[0, i, pl.ds(z + CHUNK, 1)]], axis=0)
        eyz = jnp.concatenate([ey[1:], s[1, i, pl.ds(z + CHUNK, 1)]], axis=0)
        eyx, ezx = s[1, i + 1, zs], s[2, i + 1, zs]
        hx, hy, hz = s[3, i, zs], s[4, i, zs], s[5, i, zs]
        if electric:
            hyx, hzx = s[4, i - 1, zs], s[5, i - 1, zs]
            c = coef[i - 1, pl.ds(CHUNK * k, CHUNK)]
        hx = hx + HALF * ((ahead(ez) - ez) - (eyz - ey))
        hy = hy + HALF * ((exz - ex) - (ezx - ez))
        hz = hz + HALF * ((eyx - ey) - (ahead(ex) - ex))
        s[3, i, zs] = hx
        s[4, i, zs] = hy
        s[5, i, zs] = hz
        if electric:
            put_electric(s, i, zs, c, ex, ey, ez, hx, hy, hz, hx_prev, hy_prev, hyx, hzx)
        return hx[CHUNK - 1 :], hy[CHUNK - 1 :]

    start = (s[3, i, pl.ds(0, 1)], s[4, i, pl.ds(0, 1)])
    lax.fori_loop(0, cells_z // CHUNK, chunk, start)


def put_electric(s, i, zs, c, ex, ey, ez, hx, hy, hz, hx_prev, hy_prev, hyx, hzx):
    hxz = jnp.concatenate([hx_prev, hx[:-1]], axis=0)
    hyz = jnp.concatenate([hy_prev, hy[:-1]], axis=0)
    s[0, i, zs] = ex - c * ((hz - behind(hz)) - (hy - hyz))
    s[1, i, zs] = ey - c * ((hx - hxz) - (hz - hzx))
    s[2, i, zs] = ez - c * ((hy - hyx) - (hx - behind(hx)))


def update_electric(s, coef, i, cells_z):
    def chunk(k, carry):
        hx_prev, hy_prev = carry
        zs = pl.ds(1 + CHUNK * k, CHUNK)
        ex, ey, ez = s[0, i, zs], s[1, i, zs], s[2, i, zs]
        hx, hy, hz = s[3, i, zs], s[4, i, zs], s[5, i, zs]
        hyx, hzx = s[4, i - 1, zs], s[5, i - 1, zs]
        c = coef[i - 1, pl.ds(CHUNK * k, CHUNK)]
        put_electric(s, i, zs, c, ex, ey, ez, hx, hy, hz, hx_prev, hy_prev, hyx, hzx)
        return hx[CHUNK - 1 :], hy[CHUNK - 1 :]

    start = (s[3, i, pl.ds(0, 1)], s[4, i, pl.ds(0, 1)])
    lax.fori_loop(0, cells_z // CHUNK, chunk, start)


def take_z(s, za, zb, i, even, top, cells_x, cells_z):
    j = i - 1
    right_x = jnp.where(even, za[j], zb[j])
    right_y = jnp.where(even, za[cells_x + j], zb[cells_x + j])
    left_x = jnp.where(even, zb[j], za[j])
    left_y = jnp.where(even, zb[cells_x + j], za[cells_x + j])
    s[0, i, cells_z + 1] = right_x
    s[1, i, cells_z + 1] = right_y
    s[3, i, 0] = jnp.where(top, 0.0, left_x - HALF * s[1, i, 1])
    s[4, i, 0] = jnp.where(top, 0.0, left_y + HALF * s[0, i, 1])


def inner_first_kernel(f, coef_in, za, zb, s, coef, sem):
    cells_x, cells_z = f.shape[1], f.shape[2]

    def copies(i):
        return (
            pltpu.make_async_copy(f.at[:, i], s.at[:, i + 1, pl.ds(1, cells_z)], sem.at[0, i]),
            pltpu.make_async_copy(coef_in.at[i], coef.at[i], sem.at[1, i]),
        )

    for i in range(cells_x):
        for c in copies(i):
            c.start()
    even = is_even("gz")
    top = lax.axis_index("gz") == 0

    def wait(i):
        for c in copies(i):
            c.wait()
        take_z(s, za, zb, i + 1, even, top, cells_x, cells_z)

    wait(0)
    wait(1)
    update_plane(s, coef, 1, False, cells_z)

    def plane(i, carry):
        wait(i)
        update_plane(s, coef, i, True, cells_z)
        return carry

    lax.fori_loop(2, cells_x, plane, 0)


def take_x(s, xa, xb, za, zb, cells_x, cells_z):
    even = is_even("gx")
    edge = lax.axis_index("gx") == 0
    top = lax.axis_index("gz") == 0
    last = cells_x
    for z in range(0, cells_z, 8):
        n, m, pz = pl.ds(z, 8), pl.ds(cells_z + z, 8), pl.ds(z + 1, 8)
        a0, b0, a1, b1 = xa[n], xb[n], xa[m], xb[m]
        s[1, last + 1, pz] = jnp.where(even, a0, b0)
        s[2, last + 1, pz] = jnp.where(even, a1, b1)
        hy = jnp.where(even, b0, a0) - HALF * s[2, 1, pz]
        hz = jnp.where(even, b1, a1) + HALF * s[1, 1, pz]
        s[4, 0, pz] = jnp.where(edge, 0.0, hy)
        s[5, 0, pz] = jnp.where(edge, 0.0, hz)
    corner = jnp.where(even, xa[2 * cells_z], xb[2 * cells_z])
    s[4, last, 0] = s[4, last, 0] - HALF * jnp.where(top, 0.0, corner)


def outer_planes(s, coef, cells_x, cells_z):
    update_plane(s, coef, cells_x, True, cells_z)
    update_electric(s, coef, 1, cells_z)


def edge_first_kernel(s_in, coef, xa, xb, za, zb, s, za2, zb2, xa2, xb2):
    del s_in
    cells_x, cells_z = coef.shape[0], coef.shape[1]
    take_x(s, xa, xb, za, zb, cells_x, cells_z)
    outer_planes(s, coef, cells_x, cells_z)
    xs = pl.ds(1, cells_x)
    hi = [s[c, xs, cells_z] for c in range(5)]
    z_rows(s[0, xs, 1], s[1, xs, 1], hi, za2, zb2, is_even("gz"), cells_x)
    x_rows(s.at[1:3, 1], 1, s.at[:, cells_x], xa2, xb2, is_even("gx"), cells_z)


def plane_tiles(s, plane_z, send, first, cells_x, cells_z):
    base = lax.axis_index("gz") * cells_z
    comps = 3
    for p in range(2):
        local = plane_z[p] - base
        own = (local >= 0) & (local < cells_z)
        at = 1 + jnp.clip(local, 0, cells_z - 1)
        for x in range(cells_x):
            for c in range(comps):
                v = jnp.where(own, s[c, x + 1, at], 0.0)
                send[:, first + p * comps + c, x] = v


def inner_second_kernel(s_in, coef, za, zb, plane_z, s, out, tiles, sem):
    del s_in
    cells_x, cells_z = coef.shape[0], coef.shape[1]
    even = is_even("gz")
    top = lax.axis_index("gz") == 0
    plane_tiles(s, plane_z, tiles, 0, cells_x, cells_z)

    def take(i, carry):
        take_z(s, za, zb, i, even, top, cells_x, cells_z)
        return carry

    lax.fori_loop(1, cells_x + 1, take, 0)
    inside = pl.ds(1, cells_z)

    def first():
        return pltpu.make_async_copy(s.at[3:6, 1, inside], out.at[3:6, 0], sem.at[0])

    def copy(i):
        return pltpu.make_async_copy(s.at[:, i, inside], out.at[:, i - 1], sem.at[i - 1])

    update_plane(s, coef, 1, False, cells_z)
    update_plane(s, coef, 2, True, cells_z)
    first().start()

    def plane(i, carry):
        update_plane(s, coef, i, True, cells_z)
        copy(i - 1).start()
        return carry

    lax.fori_loop(3, cells_x, plane, 0)
    copy(cells_x - 1).start()
    first().wait()

    def wait(i, carry):
        copy(i).wait()
        return carry

    lax.fori_loop(2, cells_x, wait, 0)


def edge_second_kernel(s_in, coef, xa, xb, za, zb, plane_z, out_in, tiles, s, out, send, sem):
    del s_in, out_in
    cells_x, cells_z = coef.shape[0], coef.shape[1]
    take_x(s, xa, xb, za, zb, cells_x, cells_z)
    outer_planes(s, coef, cells_x, cells_z)
    inside = pl.ds(1, cells_z)
    copies = [
        pltpu.make_async_copy(s.at[0:3, 1, inside], out.at[0:3, 0], sem.at[0]),
        pltpu.make_async_copy(s.at[:, cells_x, inside], out.at[:, cells_x - 1], sem.at[1]),
    ]
    for c in copies:
        c.start()
    for g in range(SUB):
        send[g, 0:6] = tiles[g]
    plane_tiles(s, plane_z, send, 6, cells_x, cells_z)
    per = LANE // SLOT
    comps = STEPS * 6
    for c in range(comps, send.shape[1]):
        send[:, c] = jnp.zeros_like(send[:, c])
    lane = lax.broadcasted_iota(jnp.int32, (cells_x, LANE), 1)
    for g in range(SUB):
        for k in range(comps):
            t = comps + k // per
            j = SLOT * (k % per)
            zero = jnp.zeros((cells_x, LANE), F32)
            left = send[g - 1, k] if g > 0 else zero
            right = send[g + 1, k] if g < SUB - 1 else zero
            halo = jnp.where(lane < R, right, left)
            shift = (j + R) % LANE
            moved = pltpu.roll(halo, shift, 1) if shift else halo
            send[g, t] = jnp.where((lane >= j) & (lane < j + SLOT), moved, send[g, t])
    for c in copies:
        c.wait()


def cone(pad, rows):
    width = LANE
    lane = lax.broadcasted_iota(jnp.int32, (rows, width), 1)
    own, halo = pad
    folded = []
    for v in (own, halo):
        terms = [v[R : R + rows]]
        for a in range(1, R):
            terms.append(v[R + a : R + a + rows] + v[R - a : R - a + rows])
        folded.append(terms)

    def mix(terms, b):
        acc = weight(0, b) * terms[0]
        for a in range(1, R):
            if weight(a, b) > 0.0:
                acc = acc + weight(a, b) * terms[a]
        return acc

    acc_own, acc_halo = mix(folded[0], 0), mix(folded[1], 0)
    for b in range(1, R):
        po, ph = mix(folded[0], b), mix(folded[1], b)
        o_up, h_up = pltpu.roll(po, width - b, 1), pltpu.roll(ph, width - b, 1)
        o_dn, h_dn = pltpu.roll(po, b, 1), pltpu.roll(ph, b, 1)
        keep = lane < width - b
        acc_own = acc_own + jnp.where(keep, o_up, h_up)
        acc_halo = acc_halo + jnp.where(keep, h_up, o_up)
        keep = lane >= b
        acc_own = acc_own + jnp.where(keep, o_dn, h_dn)
        acc_halo = acc_halo + jnp.where(keep, h_dn, o_dn)
    return acc_own, acc_halo


def slope_kernel(cells_x, cells_z, xa, xb, za, zb, design, slope):
    even_x, even_z = is_even("gx"), is_even("gz")
    base, n = 2 * cells_z + 1, cells_x // SUB
    zbase = 2 * cells_x + 1
    tile_a, tile_b = flat(za[pl.ds(zbase, n)]), flat(zb[pl.ds(zbase, n)])
    right = jnp.where(even_z, tile_a, tile_b)
    left = jnp.where(even_z, tile_b, tile_a)
    scale = math.tanh(SHARPNESS * THRESHOLD) + math.tanh(SHARPNESS * (1.0 - THRESHOLD))
    for p in range(2):
        middle = (design[p], unpack_slot(left, right, p))
        pads = []
        for o in range(2):
            rows = pl.ds(base + 2 * n * p + n * o, n)
            a, b = flat(xa[rows]), flat(xb[rows])
            above = jnp.where(even_x, a, b)
            below = jnp.where(even_x, b, a)
            pads.append(jnp.concatenate([below[cells_x - R :], middle[o], above[:R]], axis=0))
        for o, v in enumerate(cone(pads, cells_x)):
            t = jnp.tanh(SHARPNESS * (v - THRESHOLD))
            slope[p, o] = SHARPNESS * (1.0 - t * t) / scale


def weigh_kernel(cells_x, cells_z, recv, za, zb, sens, snaps, slope, snap_index, plane_z, wa, wb, own):
    even_x, even_z = is_even("gx"), is_even("gz")
    per = LANE // SLOT
    n = cells_x // SUB
    base = 2 * cells_x + 1
    lefts, rights = [], []
    for t in range(2):
        a, b = flat(za[pl.ds(base + n * t, n)]), flat(zb[pl.ds(base + n * t, n)])
        rights.append(jnp.where(even_z, a, b))
        lefts.append(jnp.where(even_z, b, a))
    s0 = snap_index[0]
    comps = STEPS * 6
    lane = lax.broadcasted_iota(jnp.int32, (cells_x, LANE), 1)
    edge = (lane < R) | (lane >= LANE - R)
    for p in range(2):
        owner = lax.div(plane_z[p], cells_z)
        total = sens[p]
        halo = unpack_slot(lefts[0], rights[0], 2 + p)
        for s in range(STEPS):
            acc, acc_halo = jnp.zeros_like(total), jnp.zeros_like(total)
            for c in range(3):
                k = (s * 2 + p) * 3 + c
                slot = 4 + k
                acc = acc + snaps[s0 + s, p, c] * recv[owner, k]
                tile = recv[owner, comps + k // per]
                shift = (2 * LANE - SLOT * (k % per) - R) % LANE
                field = pltpu.roll(tile, shift, 1) if shift else tile
                snap = unpack_slot(lefts[slot // per], rights[slot // per], slot % per)
                acc_halo = acc_halo + snap * field
            total = total + acc
            halo = halo + acc_halo
        w0 = total * slope[p, 0]
        w1 = jnp.where(edge, halo * slope[p, 1], 0.0)
        for o, v in enumerate((w0, w1)):
            own[p, o] = v
            up, down = v[cells_x - R :], v[:R]
            wa[p, o] = jnp.where(even_x, up, down)
            wb[p, o] = jnp.where(even_x, down, up)


def gradient_kernel(own, wa, wb, out):
    even = is_even("gx")
    cells_x = own.shape[2]
    for p in range(2):
        pads = []
        for o in range(2):
            below = jnp.where(even, wb[p, o], wa[p, o])
            above = jnp.where(even, wa[p, o], wb[p, o])
            pads.append(jnp.concatenate([below, own[p, o], above], axis=0))
        out[p] = cone(pads, cells_x)[0]


def swap(inner, outer, axis):
    size = lax.axis_size(axis)
    pairs_in = [(i, i ^ 1) for i in range(size)]
    pairs_out = [(i, i + 1 if i % 2 else i - 1) for i in range(1, size - 1)]
    far = lax.ppermute(outer, axis, pairs_out)
    near = lax.ppermute(inner, axis, pairs_in)
    return near, far


def cost(flops, nbytes):
    return pl.CostEstimate(flops=flops, bytes_accessed=nbytes, transcendentals=0)


def shards(f, coef_in, plane_z, snap_index, snaps, design, sens):
    cx, cz = f.shape[1], f.shape[2]
    zr = 2 * cx + 1
    xr = 2 * cz + 1
    extra = 2 * (cx // SUB)
    pieces = cx * SUB * LANE
    state = vmem(6, cx + 2, cz + 2, SUB, LANE)
    dma = pltpu.SemaphoreType.DMA
    field_bytes = f.size * 4

    za, zb, xa, xb = call(
        open_kernel,
        [vmem(zr + extra, SUB, LANE)] * 2 + [vmem(xr + 2 * extra, SUB, LANE)] * 2,
        (f, design, sens, snaps, snap_index),
        in_specs=[HBM, VMEM, VMEM, VMEM, SMEM],
        scratch=[
            vmem(2, cx, SUB, LANE),
            vmem(5, cx, SUB, LANE),
            vmem(2, cz, SUB, LANE),
            vmem(6, cz, SUB, LANE),
            dma((4,)),
        ],
        cost=cost(1000000, 2000000),
        limit=56,
    )
    za, zb = swap(za, zb, "gz")
    xa, xb = call(
        functools.partial(patch_kernel, cx, cz, True),
        [vmem(xr + 2 * extra, SUB, LANE)] * 2,
        (za, zb, design, xa, xb),
        alias={3: 0, 4: 1},
        cost=cost(10000, 100000),
    )
    xa, xb = swap(xa, xb, "gx")
    s, coef = call(
        inner_first_kernel,
        [state, vmem(cx, cz, SUB, LANE)],
        (f, coef_in, za, zb),
        in_specs=[HBM, HBM, VMEM, VMEM],
        scratch=[dma((2, cx))],
        cost=cost(60 * pieces * cz, 2 * field_bytes),
        limit=37,
    )
    s, za2, zb2, xa2, xb2 = call(
        edge_first_kernel,
        [state] + [vmem(zr, SUB, LANE)] * 2 + [vmem(xr, SUB, LANE)] * 2,
        (s, coef, xa, xb, za, zb),
        alias={0: 0},
        cost=cost(1000000, 2000000),
    )
    slope = call(
        functools.partial(slope_kernel, cx, cz),
        [vmem(2, 2, cx, LANE)],
        (xa, xb, za, zb, design),
        cost=cost(1000000, 100000),
    )[0]
    za2, zb2 = swap(za2, zb2, "gz")
    xa2, xb2 = call(
        functools.partial(patch_kernel, cx, cz, False),
        [vmem(xr, SUB, LANE)] * 2,
        (za2, zb2, xa2, xb2),
        alias={2: 0, 3: 1},
        cost=cost(10000, 100000),
    )
    xa2, xb2 = swap(xa2, xb2, "gx")
    tiles = STEPS * 6 + -(-STEPS * 6 * SLOT // LANE)
    s, out, first_tiles = call(
        inner_second_kernel,
        [state, jax.ShapeDtypeStruct(f.shape, F32), vmem(SUB, 6, cx, LANE)],
        (s, coef, za2, zb2, plane_z),
        in_specs=[VMEM] * 4 + [SMEM],
        out_specs=[VMEM, HBM, VMEM],
        scratch=[dma((cx,))],
        alias={0: 0},
        cost=cost(60 * pieces * cz, 2 * field_bytes),
    )
    s, out, send = call(
        edge_second_kernel,
        [state, jax.ShapeDtypeStruct(f.shape, F32), jax.ShapeDtypeStruct((SUB, tiles, cx, LANE), F32)],
        (s, coef, xa2, xb2, za2, zb2, plane_z, out, first_tiles),
        in_specs=[VMEM] * 6 + [SMEM, HBM, VMEM],
        out_specs=[VMEM, HBM, VMEM],
        scratch=[dma((2,))],
        alias={0: 0, 7: 1},
        cost=cost(1000000, 2000000),
    )
    recv = lax.all_to_all(send, "gz", 0, 0, tiled=True)
    wa, wb, own = call(
        functools.partial(weigh_kernel, cx, cz),
        [vmem(2, 2, R, LANE)] * 2 + [vmem(2, 2, cx, LANE)],
        (recv, za, zb, sens, snaps, slope, snap_index, plane_z),
        in_specs=[VMEM] * 6 + [SMEM] * 2,
        cost=cost(100000, 100000),
    )
    wa, wb = swap(wa, wb, "gx")
    gradient = call(
        gradient_kernel,
        [jax.ShapeDtypeStruct((2, cx, LANE), F32)],
        (own, wa, wb),
        cost=cost(1000000, 100000),
    )[0]
    return out, gradient


def solution(mesh):
    in_specs = (
        P(None, "gx", "gz", None, None),
        P("gx", "gz", None, None),
        P(),
        P(),
        P(None, None, None, "gx", "gz"),
        P(None, "gx", "gz"),
        P(None, "gx", "gz"),
    )
    out_specs = (P(None, "gx", "gz", None, None), P(None, "gx", "gz"))
    return jax.shard_map(shards, mesh=mesh, in_specs=in_specs, out_specs=out_specs, check_vma=False)
```

```python
import functools
import math

import jax
import jax.numpy as jnp
from jax import lax
from jax.experimental import pallas as pl
from jax.experimental.pallas import tpu as pltpu
from jax.sharding import PartitionSpec as P


R = 8
STEPS = 2
SHARPNESS = 8.0
THRESHOLD = 0.5
HALF = 0.5
F32 = jnp.float32
SUB, LANE = 8, 128
CHUNK = 32
SLOT = 16
COMPS = 6
Z_LINES = 4
X_LINES = 5

VMEM = pl.BlockSpec(memory_space=pltpu.VMEM)
HBM = pl.BlockSpec(memory_space=pltpu.HBM)
SMEM = pl.BlockSpec(memory_space=pltpu.SMEM)


def weight(a, b):
    total = sum(
        max(0.0, R - math.sqrt(i * i + j * j)) for i in range(-R, R + 1) for j in range(-R, R + 1)
    )
    return max(0.0, R - math.sqrt(a * a + b * b)) / total


def call(kernel, outs, ins, out_specs=None, in_specs=None, scratch=(), alias=None, cost=None, limit=8):
    out_specs = out_specs or [VMEM] * len(outs)
    in_specs = in_specs or [VMEM] * len(ins)
    return pl.pallas_call(
        kernel,
        out_shape=outs,
        in_specs=in_specs,
        out_specs=out_specs,
        scratch_shapes=list(scratch),
        input_output_aliases=alias or {},
        cost_estimate=cost,
        compiler_params=pltpu.CompilerParams(vmem_limit_bytes=limit << 20),
    )(*ins)


def vmem(*shape):
    return pltpu.VMEM(shape, F32)


def is_even(axis):
    return lax.rem(lax.axis_index(axis), 2) == 0


def iota(v, dim):
    return lax.broadcasted_iota(jnp.int32, v.shape, dim)


def ahead(v):
    n = v.ndim
    r = pltpu.roll(v, LANE - 1, n - 1)
    s = jnp.where(iota(v, n - 2) == SUB - 1, 0.0, pltpu.roll(r, SUB - 1, n - 2))
    return jnp.where(iota(v, n - 1) == LANE - 1, s, r)


def behind(v):
    n = v.ndim
    r = pltpu.roll(v, 1, n - 1)
    s = jnp.where(iota(v, n - 2) == 0, 0.0, pltpu.roll(r, 1, n - 2))
    return jnp.where(iota(v, n - 1) == 0, s, r)


def part_x(ex, exz, ey, ez, hy, hz):
    return hy + HALF * ((exz - ex) + ez), hz + HALF * (-ey - (ahead(ex) - ex))


def post(first, second, even, rows, forward, backward):
    first[rows] = jnp.where(even, forward, backward)
    second[rows] = jnp.where(even, backward, forward)


def pack_slots(arrays, trailing):
    per = LANE // SLOT
    tiles = []
    for t in range(-(-len(arrays) // per)):
        group = arrays[t * per : (t + 1) * per]
        lane = iota(group[0], 1)
        tile = jnp.zeros_like(group[0])
        for k, v in enumerate(group):
            shift = (SLOT * k + (SLOT if trailing else 0)) % LANE
            moved = pltpu.roll(v, shift, 1) if shift else v
            tile = jnp.where((lane >= SLOT * k) & (lane < SLOT * (k + 1)), moved, tile)
        tiles.append(tile)
    return tiles


def unpack_slot(left_tile, right_tile, k):
    lane = iota(left_tile, 1)
    right = pltpu.roll(right_tile, (LANE - SLOT * k) % LANE, 1) if k else right_tile
    shift = (LANE - SLOT - SLOT * k) % LANE
    left = pltpu.roll(left_tile, shift, 1) if shift else left_tile
    return jnp.where(lane < SLOT, right, jnp.where(lane >= LANE - SLOT, left, 0.0))


def rows_of(v):
    return v.reshape(v.shape[0] // SUB, SUB, LANE)


def flat(v):
    return v.reshape(v.shape[0] * SUB, LANE)


def open_kernel(f, coef, design, sens, snaps, snap_index, za, zb, lo, hi, post_x, ends, sem):
    cells_x, cells_z = f.shape[1], f.shape[2]
    copies = [
        pltpu.make_async_copy(f.at[0:3, :, 0], lo, sem.at[0]),
        pltpu.make_async_copy(f.at[0:5, :, cells_z - 1], hi, sem.at[1]),
        pltpu.make_async_copy(f.at[:, cells_x - 1, 0:2], post_x, sem.at[2]),
        pltpu.make_async_copy(coef.at[0, cells_z - 1], ends.at[0], sem.at[3]),
        pltpu.make_async_copy(coef.at[cells_x - 1, 0], ends.at[1], sem.at[4]),
    ]
    for c in copies:
        c.start()
    even_z = is_even("gz")
    s0 = snap_index[0]
    arrays = [design[0], design[1], sens[0], sens[1]]
    arrays += [snaps[s0 + s, p, c] for s in range(STEPS) for p in range(2) for c in range(3)]
    base = 2 * cells_x + Z_LINES
    tiles = zip(pack_slots(arrays, True), pack_slots(arrays, False))
    for t, (forward, backward) in enumerate(tiles):
        n = forward.shape[0] // SUB
        post(za, zb, even_z, pl.ds(base + n * t, n), rows_of(forward), rows_of(backward))
    for c in copies:
        c.wait()
    z_rows(lo[0], lo[1], hi, za, zb, even_z, cells_x)
    ex, ey, ez, hy, hz = (post_x[c, 0] for c in (0, 1, 2, 4, 5))
    ay, az = part_x(ex, post_x[0, 1], ey, ez, hy, hz)
    zero = jnp.zeros_like(ay)
    upward = (hi[2, 0], ends[0], zero, zero)
    downward = (lo[2, 0], ends[1], ay, az)
    for r in range(Z_LINES):
        post(za, zb, even_z, 2 * cells_x + r, upward[r], downward[r])


def open_x_kernel(f, xa, xb, first, last, sem):
    cells_x, cells_z = f.shape[1], f.shape[2]
    copies = [
        pltpu.make_async_copy(f.at[0:3, 0], first, sem.at[0]),
        pltpu.make_async_copy(f.at[:, cells_x - 1], last, sem.at[1]),
    ]
    for c in copies:
        c.start()
    for c in copies:
        c.wait()
    x_rows(first.at[1:3], 0, last, xa, xb, is_even("gx"), cells_z)
    for o in (xa, xb):
        o[2 * cells_z + X_LINES - 1] = first[0, 0]


def z_rows(ex0, ey0, hi, za, zb, even, cells_x):
    ex, ey, ez, hx, hy = (hi[c] for c in range(5))
    ez_next = jnp.concatenate([ez[1:], jnp.zeros_like(ez[:1])], axis=0)
    bx = hx + HALF * ((ahead(ez) - ez) + ey)
    by = hy + HALF * (-ex - (ez_next - ez))
    post(za, zb, even, pl.ds(0, cells_x), bx, ex0)
    post(za, zb, even, pl.ds(cells_x, cells_x), by, ey0)


def x_rows(first, offset, last, xa, xb, even, cells_z):
    for z in range(0, cells_z, 8):
        n = pl.ds(z, 8)
        ex, ey, ez, hy, hz = (last[c, pl.ds(z + offset, 8)] for c in (0, 1, 2, 4, 5))
        if z + 8 < cells_z:
            exz = last[0, pl.ds(z + offset + 1, 8)]
        else:
            exz = jnp.concatenate([ex[1:], jnp.zeros_like(ex[:1])], axis=0)
        ay, az = part_x(ex, exz, ey, ez, hy, hz)
        post(xa, xb, even, n, ay, first[0, pl.ds(z + offset, 8)])
        post(xa, xb, even, pl.ds(cells_z + z, 8), az, first[1, pl.ds(z + offset, 8)])


def patch_kernel(cells_x, cells_z, za, zb, design, xa, xb, xao, xbo):
    even_z, even_x = is_even("gz"), is_even("gx")
    for r in range(0, 2 * cells_z, 8):
        xao[pl.ds(r, 8)] = xa[pl.ds(r, 8)]
        xbo[pl.ds(r, 8)] = xb[pl.ds(r, 8)]
    above = lambda r: jnp.where(even_z, za[r], zb[r])
    below = lambda r: jnp.where(even_z, zb[r], za[r])
    line = 2 * cells_x
    ex = above(cells_x - 1)
    last = cells_z - 1
    xao[last] = xa[last] + jnp.where(even_x, HALF * ex, 0.0)
    xbo[last] = xb[last] + jnp.where(even_x, 0.0, HALF * ex)
    upward = (above(line + 2), above(line + 3), ex, above(line + 1))
    downward = (below(line), below(0), below(cells_x), below(line + 1))
    at = 2 * cells_z
    for r in range(X_LINES - 1):
        post(xao, xbo, even_x, at + r, upward[r], downward[r])
    xao[at + X_LINES - 1] = xa[at + X_LINES - 1]
    xbo[at + X_LINES - 1] = xb[at + X_LINES - 1]
    rows = at + X_LINES
    base = line + Z_LINES
    n = cells_x // SUB
    tile_a, tile_b = flat(za[pl.ds(base, n)]), flat(zb[pl.ds(base, n)])
    right = jnp.where(even_z, tile_a, tile_b)
    left = jnp.where(even_z, tile_b, tile_a)
    for p in range(2):
        own = rows_of(design[p])
        halo = rows_of(unpack_slot(left, right, p))
        for o, v in ((0, own), (n, halo)):
            xao[pl.ds(rows + 2 * n * p + o, n)] = v
            xbo[pl.ds(rows + 2 * n * p + o, n)] = v


def local_row(plane_z, p, cells_z):
    local = plane_z[p] - lax.axis_index("gz") * cells_z
    return (local >= 0) & (local < cells_z), jnp.clip(local, 0, cells_z - 1)


def update_plane(s, coef, i, electric, cells_z):
    def chunk(k, carry):
        hx_prev, hy_prev = carry
        z = 1 + CHUNK * k
        zs = pl.ds(z, CHUNK)
        ex, ey, ez = s[0, i, zs], s[1, i, zs], s[2, i, zs]
        exz = jnp.concatenate([ex[1:], s[0, i, pl.ds(z + CHUNK, 1)]], axis=0)
        eyz = jnp.concatenate([ey[1:], s[1, i, pl.ds(z + CHUNK, 1)]], axis=0)
        eyx, ezx = s[1, i + 1, zs], s[2, i + 1, zs]
        hx, hy, hz = s[3, i, zs], s[4, i, zs], s[5, i, zs]
        if electric:
            hyx, hzx = s[4, i - 1, zs], s[5, i - 1, zs]
            c = coef[i - 1, pl.ds(CHUNK * k, CHUNK)]
        hx = hx + HALF * ((ahead(ez) - ez) - (eyz - ey))
        hy = hy + HALF * ((exz - ex) - (ezx - ez))
        hz = hz + HALF * ((eyx - ey) - (ahead(ex) - ex))
        s[3, i, zs] = hx
        s[4, i, zs] = hy
        s[5, i, zs] = hz
        if electric:
            put_electric(s, i, zs, c, ex, ey, ez, hx, hy, hz, hx_prev, hy_prev, hyx, hzx)
        return hx[CHUNK - 1 :], hy[CHUNK - 1 :]

    start = (s[3, i, pl.ds(0, 1)], s[4, i, pl.ds(0, 1)])
    lax.fori_loop(0, cells_z // CHUNK, chunk, start)


def put_electric(s, i, zs, c, ex, ey, ez, hx, hy, hz, hx_prev, hy_prev, hyx, hzx):
    hxz = jnp.concatenate([hx_prev, hx[:-1]], axis=0)
    hyz = jnp.concatenate([hy_prev, hy[:-1]], axis=0)
    s[0, i, zs] = ex - c * ((hz - behind(hz)) - (hy - hyz))
    s[1, i, zs] = ey - c * ((hx - hxz) - (hz - hzx))
    s[2, i, zs] = ez - c * ((hy - hyx) - (hx - behind(hx)))


def update_electric(s, coef, i, cells_z):
    def chunk(k, carry):
        hx_prev, hy_prev = carry
        zs = pl.ds(1 + CHUNK * k, CHUNK)
        ex, ey, ez = s[0, i, zs], s[1, i, zs], s[2, i, zs]
        hx, hy, hz = s[3, i, zs], s[4, i, zs], s[5, i, zs]
        hyx, hzx = s[4, i - 1, zs], s[5, i - 1, zs]
        c = coef[i - 1, pl.ds(CHUNK * k, CHUNK)]
        put_electric(s, i, zs, c, ex, ey, ez, hx, hy, hz, hx_prev, hy_prev, hyx, hzx)
        return hx[CHUNK - 1 :], hy[CHUNK - 1 :]

    start = (s[3, i, pl.ds(0, 1)], s[4, i, pl.ds(0, 1)])
    lax.fori_loop(0, cells_z // CHUNK, chunk, start)


def take_z(s, za, zb, i, even, top, cells_x, cells_z):
    j = i - 1
    right_x = jnp.where(even, za[j], zb[j])
    right_y = jnp.where(even, za[cells_x + j], zb[cells_x + j])
    left_x = jnp.where(even, zb[j], za[j])
    left_y = jnp.where(even, zb[cells_x + j], za[cells_x + j])
    s[0, i, cells_z + 1] = right_x
    s[1, i, cells_z + 1] = right_y
    s[3, i, 0] = jnp.where(top, 0.0, left_x - HALF * s[1, i, 1])
    s[4, i, 0] = jnp.where(top, 0.0, left_y + HALF * s[0, i, 1])


def inner_first_kernel(f, coef_in, za, zb, s, coef, sem):
    cells_x, cells_z = f.shape[1], f.shape[2]

    def copies(i):
        return (
            pltpu.make_async_copy(f.at[:, i], s.at[:, i + 1, pl.ds(1, cells_z)], sem.at[0, i]),
            pltpu.make_async_copy(coef_in.at[i], coef.at[i], sem.at[1, i]),
        )

    for i in range(cells_x):
        for c in copies(i):
            c.start()
    even = is_even("gz")
    top = lax.axis_index("gz") == 0

    def wait(i):
        for c in copies(i):
            c.wait()
        take_z(s, za, zb, i + 1, even, top, cells_x, cells_z)

    wait(0)
    wait(1)
    update_plane(s, coef, 1, False, cells_z)

    def plane(i, carry):
        wait(i)
        update_plane(s, coef, i, True, cells_z)
        return carry

    lax.fori_loop(2, cells_x, plane, 0)


def take_x(s, xa, xb, corner, cells_x, cells_z):
    even = is_even("gx")
    edge = lax.axis_index("gx") == 0
    top = lax.axis_index("gz") == 0
    last = cells_x
    for z in range(0, cells_z, 8):
        n, m, pz = pl.ds(z, 8), pl.ds(cells_z + z, 8), pl.ds(z + 1, 8)
        a0, b0, a1, b1 = xa[n], xb[n], xa[m], xb[m]
        s[1, last + 1, pz] = jnp.where(even, a0, b0)
        s[2, last + 1, pz] = jnp.where(even, a1, b1)
        hy = jnp.where(even, b0, a0) - HALF * s[2, 1, pz]
        hz = jnp.where(even, b1, a1) + HALF * s[1, 1, pz]
        s[4, 0, pz] = jnp.where(edge, 0.0, hy)
        s[5, 0, pz] = jnp.where(edge, 0.0, hz)
    s[4, last, 0] = s[4, last, 0] - HALF * jnp.where(top, 0.0, corner)


def corner_lines(s, xa, xb, za, zb, cells_x, cells_z):
    even_x, even_z = is_even("gx"), is_even("gz")
    at = 2 * cells_z
    above = [jnp.where(even_x, xa[at + r], xb[at + r]) for r in range(X_LINES)]
    below = [jnp.where(even_x, xb[at + r], xa[at + r]) for r in range(X_LINES)]
    ez_next = jnp.where(even_z, za[2 * cells_x], zb[2 * cells_x])
    ay, az, ex, c = below[:4]
    hy = ay - HALF * ez_next
    hz = az + HALF * s[1, 1, cells_z + 1]
    s[0, 0, cells_z + 1] = ex - c * ((hz - behind(hz)) - (hy - s[4, 0, cells_z]))
    ez, bx, by, c, ex = above
    hx = bx - HALF * s[1, cells_x + 1, 1]
    hy = by + HALF * ex
    s[2, cells_x + 1, 0] = ez - c * ((hy - s[4, cells_x, 0]) - (hx - behind(hx)))


def outer_planes(s, coef, cells_x, cells_z):
    update_plane(s, coef, cells_x, True, cells_z)
    update_electric(s, coef, 1, cells_z)


def edge_first_kernel(s_in, coef, xa, xb, za, zb, s, za2, zb2, xa2, xb2):
    del s_in
    cells_x, cells_z = coef.shape[0], coef.shape[1]
    even = is_even("gx")
    corner = jnp.where(even, xa[2 * cells_z], xb[2 * cells_z])
    take_x(s, xa, xb, corner, cells_x, cells_z)
    corner_lines(s, xa, xb, za, zb, cells_x, cells_z)
    outer_planes(s, coef, cells_x, cells_z)
    xs = pl.ds(1, cells_x)
    hi = [s[c, xs, cells_z] for c in range(5)]
    z_rows(s[0, xs, 1], s[1, xs, 1], hi, za2, zb2, is_even("gz"), cells_x)
    x_rows(s.at[1:3, 1], 1, s.at[:, cells_x], xa2, xb2, is_even("gx"), cells_z)


def plane_tiles(s, plane_z, tiles):
    cells_x, cells_z = s.shape[1] - 2, s.shape[2] - 2
    for p in range(2):
        own, at = local_row(plane_z, p, cells_z)
        for c in range(3):
            v = jnp.where(own, s[c, pl.ds(1, cells_x), at + 1], 0.0)
            for x in range(cells_x):
                tiles[:, 3 * p + c, x] = v[x]
    lane = lax.broadcasted_iota(jnp.int32, (cells_x, LANE), 1)
    zero = jnp.zeros((cells_x, LANE), F32)
    for g in range(SUB):
        tile = zero
        for k in range(COMPS):
            left = tiles[g - 1, k] if g > 0 else zero
            right = tiles[g + 1, k] if g < SUB - 1 else zero
            halo = jnp.where(lane < R, right, left)
            moved = pltpu.roll(halo, (SLOT * k + R) % LANE, 1)
            tile = jnp.where((lane >= SLOT * k) & (lane < SLOT * (k + 1)), moved, tile)
        tiles[g, COMPS] = tile


def first_tiles_kernel(s_in, plane_z, s, tiles):
    del s_in
    plane_tiles(s, plane_z, tiles)


def inner_second_kernel(s_in, coef, za, zb, s, out, sem):
    del s_in
    cells_x, cells_z = coef.shape[0], coef.shape[1]
    inside = pl.ds(1, cells_z)
    even = is_even("gz")
    top = lax.axis_index("gz") == 0

    def take(i, carry):
        take_z(s, za, zb, i, even, top, cells_x, cells_z)
        return carry

    lax.fori_loop(1, cells_x + 1, take, 0)

    def first():
        return pltpu.make_async_copy(s.at[3:6, 1, inside], out.at[3:6, 0], sem.at[0])

    def copy(i):
        return pltpu.make_async_copy(s.at[:, i, inside], out.at[:, i - 1], sem.at[i - 1])

    update_plane(s, coef, 1, False, cells_z)
    update_plane(s, coef, 2, True, cells_z)
    first().start()

    def plane(i, carry):
        update_plane(s, coef, i, True, cells_z)
        copy(i - 1).start()
        return carry

    lax.fori_loop(3, cells_x, plane, 0)
    copy(cells_x - 1).start()
    first().wait()

    def wait(i, carry):
        copy(i).wait()
        return carry

    lax.fori_loop(2, cells_x, wait, 0)


def edge_second_kernel(s_in, coef, xa, xb, tiles, plane_z, out_in, s, out, *refs):
    del s_in, out_in
    outs, (last, sem) = refs[:SUB], refs[SUB:]
    cells_x, cells_z = coef.shape[0], coef.shape[1]
    take_x(s, xa, xb, s[2, cells_x + 1, 0], cells_x, cells_z)
    diagonal = HALF * s[0, 0, cells_z + 1]
    s[4, 0, cells_z] = s[4, 0, cells_z] + jnp.where(lax.axis_index("gx") == 0, 0.0, diagonal)
    outer_planes(s, coef, cells_x, cells_z)
    inside = pl.ds(1, cells_z)
    copies = [
        pltpu.make_async_copy(s.at[0:3, 1, inside], out.at[0:3, 0], sem.at[0]),
        pltpu.make_async_copy(s.at[:, cells_x, inside], out.at[:, cells_x - 1], sem.at[1]),
    ]
    me = lax.axis_index("gz")
    for k, o in enumerate(outs):
        o[0 : COMPS + 1] = tiles[me ^ k]
    for c in copies:
        c.start()
    plane_tiles(s, plane_z, last)
    for k, o in enumerate(outs):
        o[COMPS + 1 :] = last[me ^ k]
    for c in copies:
        c.wait()


def cone(pad, rows):
    width = LANE
    lane = lax.broadcasted_iota(jnp.int32, (rows, width), 1)
    own, halo = pad
    folded = []
    for v in (own, halo):
        terms = [v[R : R + rows]]
        for a in range(1, R):
            terms.append(v[R + a : R + a + rows] + v[R - a : R - a + rows])
        folded.append(terms)

    def mix(terms, b):
        acc = weight(0, b) * terms[0]
        for a in range(1, R):
            if weight(a, b) > 0.0:
                acc = acc + weight(a, b) * terms[a]
        return acc

    acc_own, acc_halo = mix(folded[0], 0), mix(folded[1], 0)
    for b in range(1, R):
        po, ph = mix(folded[0], b), mix(folded[1], b)
        o_up, h_up = pltpu.roll(po, width - b, 1), pltpu.roll(ph, width - b, 1)
        o_dn, h_dn = pltpu.roll(po, b, 1), pltpu.roll(ph, b, 1)
        keep = lane < width - b
        acc_own = acc_own + jnp.where(keep, o_up, h_up)
        acc_halo = acc_halo + jnp.where(keep, h_up, o_up)
        keep = lane >= b
        acc_own = acc_own + jnp.where(keep, o_dn, h_dn)
        acc_halo = acc_halo + jnp.where(keep, h_dn, o_dn)
    return acc_own, acc_halo


def slope_kernel(cells_x, cells_z, xa, xb, za, zb, design, slope):
    even_x, even_z = is_even("gx"), is_even("gz")
    base, n = 2 * cells_z + X_LINES, cells_x // SUB
    zbase = 2 * cells_x + Z_LINES
    tile_a, tile_b = flat(za[pl.ds(zbase, n)]), flat(zb[pl.ds(zbase, n)])
    right = jnp.where(even_z, tile_a, tile_b)
    left = jnp.where(even_z, tile_b, tile_a)
    scale = math.tanh(SHARPNESS * THRESHOLD) + math.tanh(SHARPNESS * (1.0 - THRESHOLD))
    for p in range(2):
        middle = (design[p], unpack_slot(left, right, p))
        pads = []
        for o in range(2):
            rows = pl.ds(base + 2 * n * p + n * o, n)
            a, b = flat(xa[rows]), flat(xb[rows])
            above = jnp.where(even_x, a, b)
            below = jnp.where(even_x, b, a)
            pads.append(jnp.concatenate([below[cells_x - R :], middle[o], above[:R]], axis=0))
        for o, v in enumerate(cone(pads, cells_x)):
            t = jnp.tanh(SHARPNESS * (v - THRESHOLD))
            slope[p, o] = SHARPNESS * (1.0 - t * t) / scale


def weigh_kernel(cells_x, cells_z, *refs):
    blocks, recv = refs[:SUB], refs[-1]
    za, zb, sens, snaps, slope, snap_index, plane_z, wa, wb, own = refs[SUB:-1]
    for p in range(2):
        sender = lax.div(plane_z[p], cells_z) ^ lax.axis_index("gz")
        for k, block in enumerate(blocks):

            @pl.when(sender == k)
            def _(block=block, p=p):
                recv[p] = block[...]

    even_x, even_z = is_even("gx"), is_even("gz")
    per = LANE // SLOT
    n = cells_x // SUB
    base = 2 * cells_x + Z_LINES
    lefts, rights = [], []
    for t in range(2):
        a, b = flat(za[pl.ds(base + n * t, n)]), flat(zb[pl.ds(base + n * t, n)])
        rights.append(jnp.where(even_z, a, b))
        lefts.append(jnp.where(even_z, b, a))
    s0 = snap_index[0]
    lane = lax.broadcasted_iota(jnp.int32, (cells_x, LANE), 1)
    edge = (lane < R) | (lane >= LANE - R)
    for p in range(2):
        total = sens[p]
        halo = unpack_slot(lefts[0], rights[0], 2 + p)
        for s in range(STEPS):
            acc, acc_halo = jnp.zeros_like(total), jnp.zeros_like(total)
            for c in range(3):
                k = p * 3 + c
                slot = 4 + s * COMPS + k
                acc = acc + snaps[s0 + s, p, c] * recv[p, s * (COMPS + 1) + k]
                tile = recv[p, s * (COMPS + 1) + COMPS]
                shift = (2 * LANE - SLOT * k - R) % LANE
                field = pltpu.roll(tile, shift, 1) if shift else tile
                snap = unpack_slot(lefts[slot // per], rights[slot // per], slot % per)
                acc_halo = acc_halo + snap * field
            total = total + acc
            halo = halo + acc_halo
        w0 = total * slope[p, 0]
        w1 = jnp.where(edge, halo * slope[p, 1], 0.0)
        for o, v in enumerate((w0, w1)):
            own[p, o] = v
            up, down = v[cells_x - R :], v[:R]
            wa[p, o] = jnp.where(even_x, up, down)
            wb[p, o] = jnp.where(even_x, down, up)


def gradient_kernel(own, wa, wb, out):
    even = is_even("gx")
    cells_x = own.shape[2]
    for p in range(2):
        pads = []
        for o in range(2):
            below = jnp.where(even, wb[p, o], wa[p, o])
            above = jnp.where(even, wa[p, o], wb[p, o])
            pads.append(jnp.concatenate([below, own[p, o], above], axis=0))
        out[p] = cone(pads, cells_x)[0]


def swap(inner, outer, axis):
    size = lax.axis_size(axis)
    pairs_in = [(i, i ^ 1) for i in range(size)]
    pairs_out = [(i, i + 1 if i % 2 else i - 1) for i in range(1, size - 1)]
    far = lax.ppermute(outer, axis, pairs_out)
    near = lax.ppermute(inner, axis, pairs_in)
    return near, far


def cost(flops, nbytes):
    return pl.CostEstimate(flops=flops, bytes_accessed=nbytes, transcendentals=0)


def shards(f, coef_in, plane_z, snap_index, snaps, design, sens):
    cx, cz = f.shape[1], f.shape[2]
    zr, xr = 2 * cx, 2 * cz
    extra = 2 * (cx // SUB)
    pieces = cx * SUB * LANE
    state = vmem(6, cx + 2, cz + 2, SUB, LANE)
    dma = pltpu.SemaphoreType.DMA
    field_bytes = f.size * 4

    za, zb = call(
        open_kernel,
        [vmem(zr + Z_LINES + extra, SUB, LANE)] * 2,
        (f, coef_in, design, sens, snaps, snap_index),
        in_specs=[HBM, HBM, VMEM, VMEM, VMEM, SMEM],
        scratch=[
            vmem(3, cx, SUB, LANE),
            vmem(5, cx, SUB, LANE),
            vmem(6, 2, SUB, LANE),
            vmem(2, SUB, LANE),
            dma((5,)),
        ],
        cost=cost(1000000, 2000000),
        limit=56,
    )
    za, zb = swap(za, zb, "gz")
    xa, xb = call(
        open_x_kernel,
        [vmem(xr + X_LINES + 2 * extra, SUB, LANE)] * 2,
        (f,),
        in_specs=[HBM],
        scratch=[vmem(3, cz, SUB, LANE), vmem(6, cz, SUB, LANE), dma((2,))],
        cost=cost(4000000, 4000000),
        limit=56,
    )
    xa, xb = call(
        functools.partial(patch_kernel, cx, cz),
        [vmem(xr + X_LINES + 2 * extra, SUB, LANE)] * 2,
        (za, zb, design, xa, xb),
        alias={3: 0, 4: 1},
        cost=cost(10000, 100000),
    )
    xa, xb = swap(xa, xb, "gx")
    s, coef = call(
        inner_first_kernel,
        [state, vmem(cx, cz, SUB, LANE)],
        (f, coef_in, za, zb),
        in_specs=[HBM, HBM, VMEM, VMEM],
        scratch=[dma((2, cx))],
        cost=cost(60 * pieces * cz, 2 * field_bytes),
        limit=37,
    )
    s, za2, zb2, xa2, xb2 = call(
        edge_first_kernel,
        [state] + [vmem(zr, SUB, LANE)] * 2 + [vmem(xr, SUB, LANE)] * 2,
        (s, coef, xa, xb, za, zb),
        alias={0: 0},
        cost=cost(1000000, 2000000),
    )
    slope = call(
        functools.partial(slope_kernel, cx, cz),
        [vmem(2, 2, cx, LANE)],
        (xa, xb, za, zb, design),
        cost=cost(1000000, 100000),
    )[0]
    za2, zb2 = swap(za2, zb2, "gz")
    s, first_tiles = call(
        first_tiles_kernel,
        [state, vmem(SUB, COMPS + 1, cx, LANE)],
        (s, plane_z),
        in_specs=[VMEM, SMEM],
        alias={0: 0},
        cost=cost(4000000, 4000000),
    )
    xa2, xb2 = swap(xa2, xb2, "gx")
    s, out = call(
        inner_second_kernel,
        [state, jax.ShapeDtypeStruct(f.shape, F32)],
        (s, coef, za2, zb2),
        in_specs=[VMEM] * 4,
        out_specs=[VMEM, HBM],
        scratch=[dma((cx,))],
        alias={0: 0},
        cost=cost(60 * pieces * cz, 2 * field_bytes),
    )
    tiles = STEPS * (COMPS + 1)
    _, out, *send = call(
        edge_second_kernel,
        [state, jax.ShapeDtypeStruct(f.shape, F32)] + [vmem(tiles, cx, LANE)] * SUB,
        (s, coef, xa2, xb2, first_tiles, plane_z, out),
        in_specs=[VMEM] * 5 + [SMEM, HBM],
        out_specs=[VMEM, HBM] + [VMEM] * SUB,
        scratch=[vmem(SUB, COMPS + 1, cx, LANE), dma((2,))],
        alias={0: 0, 6: 1},
        cost=cost(4000000, 4000000),
    )
    recv = list(send)
    for k in (6, 7, 2, 5, 3, 4, 1):
        pairs = [(i, i ^ k) for i in range(SUB)]
        recv[k] = lax.ppermute(send[k], "gz", pairs)
    wa, wb, own = call(
        functools.partial(weigh_kernel, cx, cz),
        [vmem(2, 2, R, LANE)] * 2 + [vmem(2, 2, cx, LANE)],
        (*recv, za, zb, sens, snaps, slope, snap_index, plane_z),
        in_specs=[VMEM] * (SUB + 5) + [SMEM] * 2,
        scratch=[vmem(2, tiles, cx, LANE)],
        cost=cost(100000, 100000),
    )
    wa, wb = swap(wa, wb, "gx")
    gradient = call(
        gradient_kernel,
        [jax.ShapeDtypeStruct((2, cx, LANE), F32)],
        (own, wa, wb),
        cost=cost(1000000, 100000),
    )[0]
    return out, gradient


def solution(mesh):
    in_specs = (
        P(None, "gx", "gz", None, None),
        P("gx", "gz", None, None),
        P(),
        P(),
        P(None, None, None, "gx", "gz"),
        P(None, "gx", "gz"),
        P(None, "gx", "gz"),
    )
    out_specs = (P(None, "gx", "gz", None, None), P(None, "gx", "gz"))
    return jax.shard_map(shards, mesh=mesh, in_specs=in_specs, out_specs=out_specs, check_vma=False)
```

```python
import functools
import math

import jax
import jax.numpy as jnp
from jax import lax
from jax.experimental import pallas as pl
from jax.experimental.pallas import tpu as pltpu
from jax.sharding import PartitionSpec as P


R = 8
STEPS = 2
SHARPNESS = 8.0
THRESHOLD = 0.5
HALF = 0.5
F32 = jnp.float32
SUB, LANE = 8, 128
CHUNK = 32
SLOT = 16
COMPS = 6
Z_LINES = 4
X_LINES = 5

VMEM = pl.BlockSpec(memory_space=pltpu.VMEM)
HBM = pl.BlockSpec(memory_space=pltpu.HBM)
SMEM = pl.BlockSpec(memory_space=pltpu.SMEM)


def weight(a, b):
    total = sum(
        max(0.0, R - math.sqrt(i * i + j * j)) for i in range(-R, R + 1) for j in range(-R, R + 1)
    )
    return max(0.0, R - math.sqrt(a * a + b * b)) / total


def call(kernel, outs, ins, out_specs=None, in_specs=None, scratch=(), alias=None, cost=None, limit=8):
    out_specs = out_specs or [VMEM] * len(outs)
    in_specs = in_specs or [VMEM] * len(ins)
    return pl.pallas_call(
        kernel,
        out_shape=outs,
        in_specs=in_specs,
        out_specs=out_specs,
        scratch_shapes=list(scratch),
        input_output_aliases=alias or {},
        cost_estimate=cost,
        compiler_params=pltpu.CompilerParams(vmem_limit_bytes=limit << 20),
    )(*ins)


def vmem(*shape):
    return pltpu.VMEM(shape, F32)


def is_even(axis):
    return lax.rem(lax.axis_index(axis), 2) == 0


def iota(v, dim):
    return lax.broadcasted_iota(jnp.int32, v.shape, dim)


def ahead(v):
    n = v.ndim
    r = pltpu.roll(v, LANE - 1, n - 1)
    s = jnp.where(iota(v, n - 2) == SUB - 1, 0.0, pltpu.roll(r, SUB - 1, n - 2))
    return jnp.where(iota(v, n - 1) == LANE - 1, s, r)


def behind(v):
    n = v.ndim
    r = pltpu.roll(v, 1, n - 1)
    s = jnp.where(iota(v, n - 2) == 0, 0.0, pltpu.roll(r, 1, n - 2))
    return jnp.where(iota(v, n - 1) == 0, s, r)


def part_x(ex, exz, ey, ez, hy, hz):
    return hy + HALF * ((exz - ex) + ez), hz + HALF * (-ey - (ahead(ex) - ex))


def post(first, second, even, rows, forward, backward):
    first[rows] = jnp.where(even, forward, backward)
    second[rows] = jnp.where(even, backward, forward)


def pack_slots(arrays, trailing):
    per = LANE // SLOT
    tiles = []
    for t in range(-(-len(arrays) // per)):
        group = arrays[t * per : (t + 1) * per]
        lane = iota(group[0], 1)
        tile = jnp.zeros_like(group[0])
        for k, v in enumerate(group):
            shift = (SLOT * k + (SLOT if trailing else 0)) % LANE
            moved = pltpu.roll(v, shift, 1) if shift else v
            tile = jnp.where((lane >= SLOT * k) & (lane < SLOT * (k + 1)), moved, tile)
        tiles.append(tile)
    return tiles


def unpack_slot(left_tile, right_tile, k):
    lane = iota(left_tile, 1)
    right = pltpu.roll(right_tile, (LANE - SLOT * k) % LANE, 1) if k else right_tile
    shift = (LANE - SLOT - SLOT * k) % LANE
    left = pltpu.roll(left_tile, shift, 1) if shift else left_tile
    return jnp.where(lane < SLOT, right, jnp.where(lane >= LANE - SLOT, left, 0.0))


def rows_of(v):
    return v.reshape(v.shape[0] // SUB, SUB, LANE)


def flat(v):
    return v.reshape(v.shape[0] * SUB, LANE)


def open_kernel(
    f, coef, design_in, sens_in, snaps_in, za, zb, design, sens, snaps, lo, hi, post_x, ends, sem
):
    cells_x, cells_z = f.shape[1], f.shape[2]
    copies = [
        pltpu.make_async_copy(f.at[0:3, :, 0], lo, sem.at[0]),
        pltpu.make_async_copy(f.at[0:5, :, cells_z - 1], hi, sem.at[1]),
        pltpu.make_async_copy(f.at[:, cells_x - 1, 0:2], post_x, sem.at[2]),
        pltpu.make_async_copy(coef.at[0, cells_z - 1], ends.at[0], sem.at[3]),
        pltpu.make_async_copy(coef.at[cells_x - 1, 0], ends.at[1], sem.at[4]),
        pltpu.make_async_copy(snaps_in, snaps, sem.at[5]),
        pltpu.make_async_copy(design_in, design, sem.at[6]),
        pltpu.make_async_copy(sens_in, sens, sem.at[7]),
    ]
    for c in copies:
        c.start()
    even_z = is_even("gz")
    for c in copies[5:]:
        c.wait()
    arrays = [design[0], design[1], sens[0], sens[1]]
    arrays += [snaps[s, p, c] for s in range(snaps.shape[0]) for p in range(2) for c in range(3)]
    base = 2 * cells_x + Z_LINES
    tiles = zip(pack_slots(arrays, True), pack_slots(arrays, False))
    for t, (forward, backward) in enumerate(tiles):
        n = forward.shape[0] // SUB
        post(za, zb, even_z, pl.ds(base + n * t, n), rows_of(forward), rows_of(backward))
    for c in copies[:5]:
        c.wait()
    z_rows(lo[0], lo[1], hi, za, zb, even_z, cells_x)
    ex, ey, ez, hy, hz = (post_x[c, 0] for c in (0, 1, 2, 4, 5))
    ay, az = part_x(ex, post_x[0, 1], ey, ez, hy, hz)
    zero = jnp.zeros_like(ay)
    upward = (hi[2, 0], ends[0], zero, zero)
    downward = (lo[2, 0], ends[1], ay, az)
    for r in range(Z_LINES):
        post(za, zb, even_z, 2 * cells_x + r, upward[r], downward[r])


def open_x_kernel(f, xa, xb, first, last, sem):
    cells_x, cells_z = f.shape[1], f.shape[2]
    copies = [
        pltpu.make_async_copy(f.at[0:3, 0], first, sem.at[0]),
        pltpu.make_async_copy(f.at[:, cells_x - 1], last, sem.at[1]),
    ]
    for c in copies:
        c.start()
    for c in copies:
        c.wait()
    x_rows(first.at[1:3], 0, last, xa, xb, is_even("gx"), cells_z)
    for o in (xa, xb):
        o[2 * cells_z + X_LINES - 1] = first[0, 0]


def z_rows(ex0, ey0, hi, za, zb, even, cells_x):
    ex, ey, ez, hx, hy = (hi[c] for c in range(5))
    ez_next = jnp.concatenate([ez[1:], jnp.zeros_like(ez[:1])], axis=0)
    bx = hx + HALF * ((ahead(ez) - ez) + ey)
    by = hy + HALF * (-ex - (ez_next - ez))
    post(za, zb, even, pl.ds(0, cells_x), bx, ex0)
    post(za, zb, even, pl.ds(cells_x, cells_x), by, ey0)


def x_rows(first, offset, last, xa, xb, even, cells_z):
    for z in range(0, cells_z, 8):
        n = pl.ds(z, 8)
        ex, ey, ez, hy, hz = (last[c, pl.ds(z + offset, 8)] for c in (0, 1, 2, 4, 5))
        if z + 8 < cells_z:
            exz = last[0, pl.ds(z + offset + 1, 8)]
        else:
            exz = jnp.concatenate([ex[1:], jnp.zeros_like(ex[:1])], axis=0)
        ay, az = part_x(ex, exz, ey, ez, hy, hz)
        post(xa, xb, even, n, ay, first[0, pl.ds(z + offset, 8)])
        post(xa, xb, even, pl.ds(cells_z + z, 8), az, first[1, pl.ds(z + offset, 8)])


def patch_kernel(cells_x, cells_z, za, zb, design, xa, xb, xao, xbo):
    even_z, even_x = is_even("gz"), is_even("gx")
    for r in range(0, 2 * cells_z, 8):
        xao[pl.ds(r, 8)] = xa[pl.ds(r, 8)]
        xbo[pl.ds(r, 8)] = xb[pl.ds(r, 8)]
    above = lambda r: jnp.where(even_z, za[r], zb[r])
    below = lambda r: jnp.where(even_z, zb[r], za[r])
    line = 2 * cells_x
    ex = above(cells_x - 1)
    last = cells_z - 1
    xao[last] = xa[last] + jnp.where(even_x, HALF * ex, 0.0)
    xbo[last] = xb[last] + jnp.where(even_x, 0.0, HALF * ex)
    upward = (above(line + 2), above(line + 3), ex, above(line + 1))
    downward = (below(line), below(0), below(cells_x), below(line + 1))
    at = 2 * cells_z
    for r in range(X_LINES - 1):
        post(xao, xbo, even_x, at + r, upward[r], downward[r])
    xao[at + X_LINES - 1] = xa[at + X_LINES - 1]
    xbo[at + X_LINES - 1] = xb[at + X_LINES - 1]
    rows = at + X_LINES
    base = line + Z_LINES
    n = cells_x // SUB
    tile_a, tile_b = flat(za[pl.ds(base, n)]), flat(zb[pl.ds(base, n)])
    right = jnp.where(even_z, tile_a, tile_b)
    left = jnp.where(even_z, tile_b, tile_a)
    for p in range(2):
        own = rows_of(design[p])
        halo = rows_of(unpack_slot(left, right, p))
        for o, v in ((0, own), (n, halo)):
            xao[pl.ds(rows + 2 * n * p + o, n)] = v
            xbo[pl.ds(rows + 2 * n * p + o, n)] = v


def local_row(plane_z, p, cells_z):
    local = plane_z[p] - lax.axis_index("gz") * cells_z
    return (local >= 0) & (local < cells_z), jnp.clip(local, 0, cells_z - 1)


def update_plane(s, coef, i, electric, cells_z):
    def chunk(k, carry):
        hx_prev, hy_prev = carry
        z = 1 + CHUNK * k
        zs = pl.ds(z, CHUNK)
        ex, ey, ez = s[0, i, zs], s[1, i, zs], s[2, i, zs]
        exz = jnp.concatenate([ex[1:], s[0, i, pl.ds(z + CHUNK, 1)]], axis=0)
        eyz = jnp.concatenate([ey[1:], s[1, i, pl.ds(z + CHUNK, 1)]], axis=0)
        eyx, ezx = s[1, i + 1, zs], s[2, i + 1, zs]
        hx, hy, hz = s[3, i, zs], s[4, i, zs], s[5, i, zs]
        if electric:
            hyx, hzx = s[4, i - 1, zs], s[5, i - 1, zs]
            c = coef[i - 1, pl.ds(CHUNK * k, CHUNK)]
        hx = hx + HALF * ((ahead(ez) - ez) - (eyz - ey))
        hy = hy + HALF * ((exz - ex) - (ezx - ez))
        hz = hz + HALF * ((eyx - ey) - (ahead(ex) - ex))
        s[3, i, zs] = hx
        s[4, i, zs] = hy
        s[5, i, zs] = hz
        if electric:
            put_electric(s, i, zs, c, ex, ey, ez, hx, hy, hz, hx_prev, hy_prev, hyx, hzx)
        return hx[CHUNK - 1 :], hy[CHUNK - 1 :]

    start = (s[3, i, pl.ds(0, 1)], s[4, i, pl.ds(0, 1)])
    lax.fori_loop(0, cells_z // CHUNK, chunk, start)


def put_electric(s, i, zs, c, ex, ey, ez, hx, hy, hz, hx_prev, hy_prev, hyx, hzx):
    hxz = jnp.concatenate([hx_prev, hx[:-1]], axis=0)
    hyz = jnp.concatenate([hy_prev, hy[:-1]], axis=0)
    s[0, i, zs] = ex - c * ((hz - behind(hz)) - (hy - hyz))
    s[1, i, zs] = ey - c * ((hx - hxz) - (hz - hzx))
    s[2, i, zs] = ez - c * ((hy - hyx) - (hx - behind(hx)))


def update_electric(s, coef, i, cells_z):
    def chunk(k, carry):
        hx_prev, hy_prev = carry
        zs = pl.ds(1 + CHUNK * k, CHUNK)
        ex, ey, ez = s[0, i, zs], s[1, i, zs], s[2, i, zs]
        hx, hy, hz = s[3, i, zs], s[4, i, zs], s[5, i, zs]
        hyx, hzx = s[4, i - 1, zs], s[5, i - 1, zs]
        c = coef[i - 1, pl.ds(CHUNK * k, CHUNK)]
        put_electric(s, i, zs, c, ex, ey, ez, hx, hy, hz, hx_prev, hy_prev, hyx, hzx)
        return hx[CHUNK - 1 :], hy[CHUNK - 1 :]

    start = (s[3, i, pl.ds(0, 1)], s[4, i, pl.ds(0, 1)])
    lax.fori_loop(0, cells_z // CHUNK, chunk, start)


def take_z(s, za, zb, i, even, top, cells_x, cells_z):
    j = i - 1
    right_x = jnp.where(even, za[j], zb[j])
    right_y = jnp.where(even, za[cells_x + j], zb[cells_x + j])
    left_x = jnp.where(even, zb[j], za[j])
    left_y = jnp.where(even, zb[cells_x + j], za[cells_x + j])
    s[0, i, cells_z + 1] = right_x
    s[1, i, cells_z + 1] = right_y
    s[3, i, 0] = jnp.where(top, 0.0, left_x - HALF * s[1, i, 1])
    s[4, i, 0] = jnp.where(top, 0.0, left_y + HALF * s[0, i, 1])


def inner_first_kernel(f, coef_in, za, zb, s, coef, sem):
    cells_x, cells_z = f.shape[1], f.shape[2]

    def copies(i):
        return (
            pltpu.make_async_copy(f.at[:, i], s.at[:, i + 1, pl.ds(1, cells_z)], sem.at[0, i]),
            pltpu.make_async_copy(coef_in.at[i], coef.at[i], sem.at[1, i]),
        )

    for i in range(cells_x):
        for c in copies(i):
            c.start()
    even = is_even("gz")
    top = lax.axis_index("gz") == 0

    def wait(i):
        for c in copies(i):
            c.wait()
        take_z(s, za, zb, i + 1, even, top, cells_x, cells_z)

    wait(0)
    wait(1)
    update_plane(s, coef, 1, False, cells_z)

    def plane(i, carry):
        wait(i)
        update_plane(s, coef, i, True, cells_z)
        return carry

    lax.fori_loop(2, cells_x, plane, 0)


def take_x(s, xa, xb, corner, cells_x, cells_z):
    even = is_even("gx")
    edge = lax.axis_index("gx") == 0
    top = lax.axis_index("gz") == 0
    last = cells_x
    for z in range(0, cells_z, 8):
        n, m, pz = pl.ds(z, 8), pl.ds(cells_z + z, 8), pl.ds(z + 1, 8)
        a0, b0, a1, b1 = xa[n], xb[n], xa[m], xb[m]
        s[1, last + 1, pz] = jnp.where(even, a0, b0)
        s[2, last + 1, pz] = jnp.where(even, a1, b1)
        hy = jnp.where(even, b0, a0) - HALF * s[2, 1, pz]
        hz = jnp.where(even, b1, a1) + HALF * s[1, 1, pz]
        s[4, 0, pz] = jnp.where(edge, 0.0, hy)
        s[5, 0, pz] = jnp.where(edge, 0.0, hz)
    s[4, last, 0] = s[4, last, 0] - HALF * jnp.where(top, 0.0, corner)


def corner_lines(s, xa, xb, za, zb, cells_x, cells_z):
    even_x, even_z = is_even("gx"), is_even("gz")
    at = 2 * cells_z
    above = [jnp.where(even_x, xa[at + r], xb[at + r]) for r in range(X_LINES)]
    below = [jnp.where(even_x, xb[at + r], xa[at + r]) for r in range(X_LINES)]
    ez_next = jnp.where(even_z, za[2 * cells_x], zb[2 * cells_x])
    ay, az, ex, c = below[:4]
    hy = ay - HALF * ez_next
    hz = az + HALF * s[1, 1, cells_z + 1]
    s[0, 0, cells_z + 1] = ex - c * ((hz - behind(hz)) - (hy - s[4, 0, cells_z]))
    ez, bx, by, c, ex = above
    hx = bx - HALF * s[1, cells_x + 1, 1]
    hy = by + HALF * ex
    s[2, cells_x + 1, 0] = ez - c * ((hy - s[4, cells_x, 0]) - (hx - behind(hx)))


def outer_planes(s, coef, cells_x, cells_z):
    update_plane(s, coef, cells_x, True, cells_z)
    update_electric(s, coef, 1, cells_z)


def edge_first_kernel(s_in, coef, xa, xb, za, zb, s, za2, zb2, xa2, xb2):
    del s_in
    cells_x, cells_z = coef.shape[0], coef.shape[1]
    even = is_even("gx")
    corner = jnp.where(even, xa[2 * cells_z], xb[2 * cells_z])
    take_x(s, xa, xb, corner, cells_x, cells_z)
    corner_lines(s, xa, xb, za, zb, cells_x, cells_z)
    outer_planes(s, coef, cells_x, cells_z)
    xs = pl.ds(1, cells_x)
    hi = [s[c, xs, cells_z] for c in range(5)]
    z_rows(s[0, xs, 1], s[1, xs, 1], hi, za2, zb2, is_even("gz"), cells_x)
    x_rows(s.at[1:3, 1], 1, s.at[:, cells_x], xa2, xb2, is_even("gx"), cells_z)


def plane_tiles(s, plane_z, tiles):
    cells_x, cells_z = s.shape[1] - 2, s.shape[2] - 2
    for p in range(2):
        own, at = local_row(plane_z, p, cells_z)
        for c in range(3):
            v = jnp.where(own, s[c, pl.ds(1, cells_x), at + 1], 0.0)
            for x in range(cells_x):
                tiles[:, 3 * p + c, x] = v[x]
    lane = lax.broadcasted_iota(jnp.int32, (cells_x, LANE), 1)
    zero = jnp.zeros((cells_x, LANE), F32)
    for g in range(SUB):
        tile = zero
        for k in range(COMPS):
            left = tiles[g - 1, k] if g > 0 else zero
            right = tiles[g + 1, k] if g < SUB - 1 else zero
            halo = jnp.where(lane < R, right, left)
            moved = pltpu.roll(halo, (SLOT * k + R) % LANE, 1)
            tile = jnp.where((lane >= SLOT * k) & (lane < SLOT * (k + 1)), moved, tile)
        tiles[g, COMPS] = tile


def first_tiles_kernel(s_in, plane_z, s, tiles):
    del s_in
    plane_tiles(s, plane_z, tiles)


def inner_second_kernel(s_in, coef, za, zb, s, out, sem):
    del s_in
    cells_x, cells_z = coef.shape[0], coef.shape[1]
    inside = pl.ds(1, cells_z)
    even = is_even("gz")
    top = lax.axis_index("gz") == 0

    def take(i, carry):
        take_z(s, za, zb, i, even, top, cells_x, cells_z)
        return carry

    lax.fori_loop(1, cells_x + 1, take, 0)

    def first():
        return pltpu.make_async_copy(s.at[3:6, 1, inside], out.at[3:6, 0], sem.at[0])

    def copy(i):
        return pltpu.make_async_copy(s.at[:, i, inside], out.at[:, i - 1], sem.at[i - 1])

    update_plane(s, coef, 1, False, cells_z)
    update_plane(s, coef, 2, True, cells_z)
    first().start()

    def plane(i, carry):
        update_plane(s, coef, i, True, cells_z)
        copy(i - 1).start()
        return carry

    lax.fori_loop(3, cells_x, plane, 0)
    copy(cells_x - 1).start()
    first().wait()

    def wait(i, carry):
        copy(i).wait()
        return carry

    lax.fori_loop(2, cells_x, wait, 0)


def edge_second_kernel(s_in, coef, xa, xb, tiles, plane_z, out_in, s, out, *refs):
    del s_in, out_in
    outs, (last, sem) = refs[:SUB], refs[SUB:]
    cells_x, cells_z = coef.shape[0], coef.shape[1]
    take_x(s, xa, xb, s[2, cells_x + 1, 0], cells_x, cells_z)
    diagonal = HALF * s[0, 0, cells_z + 1]
    s[4, 0, cells_z] = s[4, 0, cells_z] + jnp.where(lax.axis_index("gx") == 0, 0.0, diagonal)
    outer_planes(s, coef, cells_x, cells_z)
    inside = pl.ds(1, cells_z)
    copies = [
        pltpu.make_async_copy(s.at[0:3, 1, inside], out.at[0:3, 0], sem.at[0]),
        pltpu.make_async_copy(s.at[:, cells_x, inside], out.at[:, cells_x - 1], sem.at[1]),
    ]
    me = lax.axis_index("gz")
    for k, o in enumerate(outs):
        o[0 : COMPS + 1] = tiles[me ^ k]
    for c in copies:
        c.start()
    plane_tiles(s, plane_z, last)
    for k, o in enumerate(outs):
        o[COMPS + 1 :] = last[me ^ k]
    for c in copies:
        c.wait()


def cone(pad, rows):
    width = LANE
    lane = lax.broadcasted_iota(jnp.int32, (rows, width), 1)
    own, halo = pad
    folded = []
    for v in (own, halo):
        terms = [v[R : R + rows]]
        for a in range(1, R):
            terms.append(v[R + a : R + a + rows] + v[R - a : R - a + rows])
        folded.append(terms)

    def mix(terms, b):
        acc = weight(0, b) * terms[0]
        for a in range(1, R):
            if weight(a, b) > 0.0:
                acc = acc + weight(a, b) * terms[a]
        return acc

    acc_own, acc_halo = mix(folded[0], 0), mix(folded[1], 0)
    for b in range(1, R):
        po, ph = mix(folded[0], b), mix(folded[1], b)
        o_up, h_up = pltpu.roll(po, width - b, 1), pltpu.roll(ph, width - b, 1)
        o_dn, h_dn = pltpu.roll(po, b, 1), pltpu.roll(ph, b, 1)
        keep = lane < width - b
        acc_own = acc_own + jnp.where(keep, o_up, h_up)
        acc_halo = acc_halo + jnp.where(keep, h_up, o_up)
        keep = lane >= b
        acc_own = acc_own + jnp.where(keep, o_dn, h_dn)
        acc_halo = acc_halo + jnp.where(keep, h_dn, o_dn)
    return acc_own, acc_halo


def slope_kernel(
    cells_x, cells_z, xa, xb, za, zb, design, snaps, snap_index, slope, pair, pair_halo, halos
):
    even_x, even_z = is_even("gx"), is_even("gz")
    base, n = 2 * cells_z + X_LINES, cells_x // SUB
    zbase = 2 * cells_x + Z_LINES
    tile_a, tile_b = flat(za[pl.ds(zbase, n)]), flat(zb[pl.ds(zbase, n)])
    right = jnp.where(even_z, tile_a, tile_b)
    left = jnp.where(even_z, tile_b, tile_a)
    per = LANE // SLOT
    steps = snaps.shape[0]
    for t in range(-(-(4 + COMPS * steps) // per)):
        a, b = flat(za[pl.ds(zbase + n * t, n)]), flat(zb[pl.ds(zbase + n * t, n)])
        above, below = jnp.where(even_z, a, b), jnp.where(even_z, b, a)
        for slot in range(max(4, per * t), min(4 + COMPS * steps, per * (t + 1))):
            s, k = divmod(slot - 4, COMPS)
            halos[s, k // 3, k % 3] = unpack_slot(below, above, slot % per)
    for s in range(STEPS):
        pair[s] = snaps[snap_index[0] + s]
        pair_halo[s] = halos[snap_index[0] + s]
    scale = math.tanh(SHARPNESS * THRESHOLD) + math.tanh(SHARPNESS * (1.0 - THRESHOLD))
    for p in range(2):
        middle = (design[p], unpack_slot(left, right, p))
        pads = []
        for o in range(2):
            rows = pl.ds(base + 2 * n * p + n * o, n)
            a, b = flat(xa[rows]), flat(xb[rows])
            above = jnp.where(even_x, a, b)
            below = jnp.where(even_x, b, a)
            pads.append(jnp.concatenate([below[cells_x - R :], middle[o], above[:R]], axis=0))
        for o, v in enumerate(cone(pads, cells_x)):
            t = jnp.tanh(SHARPNESS * (v - THRESHOLD))
            slope[p, o] = SHARPNESS * (1.0 - t * t) / scale


def weigh_kernel(cells_x, cells_z, *refs):
    blocks, recv = refs[:SUB], refs[-1]
    za, zb, sens, pair, pair_halo, slope, plane_z, wa, wb, own = refs[SUB:-1]
    for p in range(2):
        sender = lax.div(plane_z[p], cells_z) ^ lax.axis_index("gz")
        for k, block in enumerate(blocks):

            @pl.when(sender == k)
            def _(block=block, p=p):
                recv[p] = block[...]

    even_x, even_z = is_even("gx"), is_even("gz")
    n = cells_x // SUB
    first = pl.ds(2 * cells_x + Z_LINES, n)
    a, b = flat(za[first]), flat(zb[first])
    right, left = jnp.where(even_z, a, b), jnp.where(even_z, b, a)
    lane = lax.broadcasted_iota(jnp.int32, (cells_x, LANE), 1)
    edge = (lane < R) | (lane >= LANE - R)
    for p in range(2):
        total = sens[p]
        halo = unpack_slot(left, right, 2 + p)
        for s in range(STEPS):
            acc, acc_halo = jnp.zeros_like(total), jnp.zeros_like(total)
            for c in range(3):
                k = p * 3 + c
                acc = acc + pair[s, p, c] * recv[p, s * (COMPS + 1) + k]
                tile = recv[p, s * (COMPS + 1) + COMPS]
                shift = (2 * LANE - SLOT * k - R) % LANE
                field = pltpu.roll(tile, shift, 1) if shift else tile
                acc_halo = acc_halo + pair_halo[s, p, c] * field
            total = total + acc
            halo = halo + acc_halo
        w0 = total * slope[p, 0]
        w1 = jnp.where(edge, halo * slope[p, 1], 0.0)
        for o, v in enumerate((w0, w1)):
            own[p, o] = v
            up, down = v[cells_x - R :], v[:R]
            wa[p, o] = jnp.where(even_x, up, down)
            wb[p, o] = jnp.where(even_x, down, up)


def gradient_kernel(own, wa, wb, out):
    even = is_even("gx")
    cells_x = own.shape[2]
    for p in range(2):
        pads = []
        for o in range(2):
            below = jnp.where(even, wb[p, o], wa[p, o])
            above = jnp.where(even, wa[p, o], wb[p, o])
            pads.append(jnp.concatenate([below, own[p, o], above], axis=0))
        out[p] = cone(pads, cells_x)[0]


def swap(inner, outer, axis):
    size = lax.axis_size(axis)
    pairs_in = [(i, i ^ 1) for i in range(size)]
    pairs_out = [(i, i + 1 if i % 2 else i - 1) for i in range(1, size - 1)]
    far = lax.ppermute(outer, axis, pairs_out)
    near = lax.ppermute(inner, axis, pairs_in)
    return near, far


def cost(flops, nbytes):
    return pl.CostEstimate(flops=flops, bytes_accessed=nbytes, transcendentals=0)


def shards(f, coef_in, plane_z, snap_index, snaps, design, sens):
    cx, cz = f.shape[1], f.shape[2]
    zr, xr = 2 * cx, 2 * cz
    extra = 2 * (cx // SUB)
    pieces = cx * SUB * LANE
    state = vmem(6, cx + 2, cz + 2, SUB, LANE)
    dma = pltpu.SemaphoreType.DMA
    field_bytes = f.size * 4

    selected = (STEPS,) + snaps.shape[1:]
    z_extra = -(-(4 + COMPS * snaps.shape[0]) * SLOT // LANE) * (cx // SUB)
    za, zb, design, sens, snaps = call(
        open_kernel,
        [vmem(zr + Z_LINES + z_extra, SUB, LANE)] * 2
        + [vmem(*design.shape), vmem(*sens.shape), vmem(*snaps.shape)],
        (f, coef_in, design, sens, snaps),
        in_specs=[HBM] * 5,
        scratch=[
            vmem(3, cx, SUB, LANE),
            vmem(5, cx, SUB, LANE),
            vmem(6, 2, SUB, LANE),
            vmem(2, SUB, LANE),
            dma((8,)),
        ],
        cost=cost(1000000, 2000000),
        limit=56,
    )
    za, zb = swap(za, zb, "gz")
    xa, xb = call(
        open_x_kernel,
        [vmem(xr + X_LINES + 2 * extra, SUB, LANE)] * 2,
        (f,),
        in_specs=[HBM],
        scratch=[vmem(3, cz, SUB, LANE), vmem(6, cz, SUB, LANE), dma((2,))],
        cost=cost(4000000, 4000000),
        limit=56,
    )
    xa, xb = call(
        functools.partial(patch_kernel, cx, cz),
        [vmem(xr + X_LINES + 2 * extra, SUB, LANE)] * 2,
        (za, zb, design, xa, xb),
        alias={3: 0, 4: 1},
        cost=cost(10000, 100000),
    )
    xa, xb = swap(xa, xb, "gx")
    s, coef = call(
        inner_first_kernel,
        [state, vmem(cx, cz, SUB, LANE)],
        (f, coef_in, za, zb),
        in_specs=[HBM, HBM, VMEM, VMEM],
        scratch=[dma((2, cx))],
        cost=cost(60 * pieces * cz, 2 * field_bytes),
        limit=37,
    )
    s, za2, zb2, xa2, xb2 = call(
        edge_first_kernel,
        [state] + [vmem(zr, SUB, LANE)] * 2 + [vmem(xr, SUB, LANE)] * 2,
        (s, coef, xa, xb, za, zb),
        alias={0: 0},
        cost=cost(1000000, 2000000),
    )
    slope, pair, pair_halo = call(
        functools.partial(slope_kernel, cx, cz),
        [vmem(2, 2, cx, LANE), vmem(*selected), vmem(*selected)],
        (xa, xb, za, zb, design, snaps, snap_index),
        in_specs=[VMEM] * 6 + [SMEM],
        scratch=[vmem(*snaps.shape)],
        cost=cost(1000000, 100000),
    )
    za2, zb2 = swap(za2, zb2, "gz")
    s, first_tiles = call(
        first_tiles_kernel,
        [state, vmem(SUB, COMPS + 1, cx, LANE)],
        (s, plane_z),
        in_specs=[VMEM, SMEM],
        alias={0: 0},
        cost=cost(4000000, 4000000),
    )
    xa2, xb2 = swap(xa2, xb2, "gx")
    s, out = call(
        inner_second_kernel,
        [state, jax.ShapeDtypeStruct(f.shape, F32)],
        (s, coef, za2, zb2),
        in_specs=[VMEM] * 4,
        out_specs=[VMEM, HBM],
        scratch=[dma((cx,))],
        alias={0: 0},
        cost=cost(60 * pieces * cz, 2 * field_bytes),
    )
    tiles = STEPS * (COMPS + 1)
    _, out, *send = call(
        edge_second_kernel,
        [state, jax.ShapeDtypeStruct(f.shape, F32)] + [vmem(tiles, cx, LANE)] * SUB,
        (s, coef, xa2, xb2, first_tiles, plane_z, out),
        in_specs=[VMEM] * 5 + [SMEM, HBM],
        out_specs=[VMEM, HBM] + [VMEM] * SUB,
        scratch=[vmem(SUB, COMPS + 1, cx, LANE), dma((2,))],
        alias={0: 0, 6: 1},
        cost=cost(4000000, 4000000),
    )
    recv = list(send)
    for k in (6, 7, 2, 5, 3, 4, 1):
        pairs = [(i, i ^ k) for i in range(SUB)]
        recv[k] = lax.ppermute(send[k], "gz", pairs)
    wa, wb, own = call(
        functools.partial(weigh_kernel, cx, cz),
        [vmem(2, 2, R, LANE)] * 2 + [vmem(2, 2, cx, LANE)],
        (*recv, za, zb, sens, pair, pair_halo, slope, plane_z),
        in_specs=[VMEM] * (SUB + 6) + [SMEM],
        scratch=[vmem(2, tiles, cx, LANE)],
        cost=cost(100000, 100000),
    )
    wa, wb = swap(wa, wb, "gx")
    gradient = call(
        gradient_kernel,
        [jax.ShapeDtypeStruct((2, cx, LANE), F32)],
        (own, wa, wb),
        cost=cost(1000000, 100000),
    )[0]
    return out, gradient


def solution(mesh):
    in_specs = (
        P(None, "gx", "gz", None, None),
        P("gx", "gz", None, None),
        P(),
        P(),
        P(None, None, None, "gx", "gz"),
        P(None, "gx", "gz"),
        P(None, "gx", "gz"),
    )
    out_specs = (P(None, "gx", "gz", None, None), P(None, "gx", "gz"))
    return jax.shard_map(shards, mesh=mesh, in_specs=in_specs, out_specs=out_specs, check_vma=False)
```
